32 devices in a mesh: shot: 2 (over x), gx: 16 (over z, y, core).
Axes of the slice: x: 2, y: 2, z: 4, core: 2. Of those that a mesh axis runs over, the one named last changes fastest.
Arguments:
- waves_now: float32 [2, 1024, 64, 128], P(None, ('shot', 'gx')), parts along dimension 1, may hold values from -6 to 6
- waves_prev: float32 [2, 1024, 64, 128], P(None, ('shot', 'gx')), parts along dimension 1, may hold values from -6 to 6
- epsilon: bfloat16 [512, 64, 128], P('gx'), may hold values from 0.049804688 to 0.3984375
- tilt: bfloat16 [512, 64, 128], P('gx'), may hold values from -3.140625 to 3.140625
- azimuth: bfloat16 [512, 64, 128], P('gx'), may hold values from -3.140625 to 3.140625
- courant: bfloat16 [512, 64, 128], P('gx'), may hold values from 0.029907227 to 0.099609375
- lag_offsets: int32 [32], replicated, may hold values from -16 to 15
- table_index: int32 [128], replicated, may hold values from 0 to 3
- lag_tables: bfloat16 [4, 32, 32], replicated, may hold values from -1 to 1
Outputs:
- angle_image: bfloat16 [32, 8192, 256], P(None, ('shot', 'gx')), parts along dimension 1
The draws below stay inside these ranges and needn't reach their ends.
There are 2 independent parts, one for each index of `shot`. The reference program is written for one: setup_inputs(seed, part) draws one part's arguments, and reference() takes and returns one part's arrays. A program takes and returns all parts, laid end to end along the dimension named above; an argument that names none is the same for every part. Nothing has to cross between parts.
All inputs are finite; a program needn't handle non-finite values.
Results may differ from the reference program's by a relative error of at most 0.0049.
Values may be sent and summed in bfloat16 or wider, within the bound.
A program may use at most 64 MiB of HBM per device.

```python
import math
import jax
import jax.numpy as jnp
from jax import lax

NY = 64
NZ = 128
STEPS = 4
LAGS = 32
ANGLES = 32
LAG_REACH = 16
TABLES = 4
NX = 512


def plant(entries, rng, smallest, high):
    longest = entries.shape.index(max(entries.shape))
    spots = []
    for shift in (0, 1):
        where = [jax.random.randint(jax.random.fold_in(rng, axis), (), 0, length) for axis, length in enumerate(entries.shape)]
        where[longest] = (where[longest] + shift) % entries.shape[longest]
        spots.append(tuple(where))
    return entries.at[spots[0]].set(smallest).at[spots[1]].set(high)


def shard_levels(stream_key, dims, split, smallest, high):
    level, own = 1.0, jax.random.fold_in(stream_key, 6)
    for dim, blocks in split:
        heights = jnp.exp(jax.random.uniform(jax.random.fold_in(own, dim), (blocks,), jnp.float32, smallest / len(split), high / len(split)))
        level = level * jnp.repeat(heights, dims[dim] // blocks).reshape([-1 if axis == dim else 1 for axis in range(len(dims))])
    return level


def centred(rng, extent, spread, most, cuts=(), kind=jnp.bfloat16):
    factor_of = shard_levels(rng, extent, cuts, -0.22, 0.18) if cuts else 1.0
    array = jax.random.normal(rng, extent, jnp.float32) * spread * factor_of
    return jnp.minimum(jnp.maximum(array, -most), most).astype(kind)


def setup_inputs(seed: int = 0, part: int = 0) -> dict:
    splits = jax.random.split(jax.random.key(seed), 10)
    part_splits = jax.random.split(jax.random.fold_in(splits[9], part), 10)
    waves_now = centred(part_splits[0], (2, NX, NY, NZ), 1.0, 6.0, ((1, 16),), jnp.float32)
    waves_prev = centred(part_splits[1], (2, NX, NY, NZ), 1.0, 6.0, ((1, 16),), jnp.float32)
    epsilon = jnp.clip(0.049804688 + 0.3486328 * jax.random.uniform(splits[2], (NX, NY, NZ), jnp.float32) ** shard_levels(splits[2], (NX, NY, NZ), ((0, 16),), -0.2, 0.2), 0.049804688, 0.3984375).astype(jnp.bfloat16)
    tilt = jnp.clip(jax.random.uniform(splits[3], (NX, NY, NZ), jnp.float32, -3.140625, 3.140625), -3.140625, 3.140625).astype(jnp.bfloat16)
    azimuth = jnp.clip(jax.random.uniform(splits[4], (NX, NY, NZ), jnp.float32, -3.140625, 3.140625), -3.140625, 3.140625).astype(jnp.bfloat16)
    courant = jnp.clip(jnp.exp(math.log(0.099609375) - 1.2031561 * jax.random.uniform(splits[5], (NX, NY, NZ), jnp.float32) ** shard_levels(splits[5], (NX, NY, NZ), ((0, 16),), -0.2, 0.2)), 0.029907227, 0.099609375).astype(jnp.bfloat16)
    lag_offsets = plant(jax.random.randint(splits[6], (LAGS,), 0 - LAG_REACH, LAG_REACH), jax.random.fold_in(splits[6], 1), 0 - LAG_REACH, LAG_REACH - 1).astype(jnp.int32)
    table_index = plant(jax.random.randint(splits[7], (NZ,), 0, TABLES), jax.random.fold_in(splits[7], 1), 0, TABLES - 1).astype(jnp.int32)
    lag_tables = centred(splits[8], (TABLES, ANGLES, LAGS), LAGS ** -0.5, 1.0)
    return {"waves_now": waves_now, "waves_prev": waves_prev, "epsilon": epsilon, "tilt": tilt, "azimuth": azimuth, "courant": courant, "lag_offsets": lag_offsets, "table_index": table_index, "lag_tables": lag_tables}


def tensor(epsilon, tilt, azimuth, courant):
    eps = epsilon.astype(jnp.float32)
    theta = tilt.astype(jnp.float32)
    alpha = azimuth.astype(jnp.float32)
    speed = courant.astype(jnp.float32)
    axis_x = jnp.sin(theta) * jnp.cos(alpha)
    axis_y = jnp.sin(theta) * jnp.sin(alpha)
    axis_z = jnp.cos(theta)
    base = speed * (1.0 + 2.0 * eps)
    scaled = speed * 2.0 * eps
    return (base - scaled * axis_x * axis_x, base - scaled * axis_y * axis_y, base - scaled * axis_z * axis_z,
            -scaled * axis_x * axis_y, -scaled * axis_x * axis_z, -scaled * axis_y * axis_z)


def laplace(extended, comps):
    inner = extended.shape[1] - 2
    depth_y = extended.shape[2]
    depth_z = extended.shape[3]
    padded = jnp.pad(extended, ((0, 0), (0, 0), (1, 1), (1, 1)))

    def shifted(dx, dy, dz):
        return padded[:, 1 + dx:1 + dx + inner, 1 + dy:1 + dy + depth_y, 1 + dz:1 + dz + depth_z]

    center = shifted(0, 0, 0)
    d_xx = shifted(1, 0, 0) - 2.0 * center + shifted(-1, 0, 0)
    d_yy = shifted(0, 1, 0) - 2.0 * center + shifted(0, -1, 0)
    d_zz = shifted(0, 0, 1) - 2.0 * center + shifted(0, 0, -1)
    d_xy = shifted(1, 1, 0) - shifted(1, -1, 0) - shifted(-1, 1, 0) + shifted(-1, -1, 0)
    d_xz = shifted(1, 0, 1) - shifted(1, 0, -1) - shifted(-1, 0, 1) + shifted(-1, 0, -1)
    d_yz = shifted(0, 1, 1) - shifted(0, 1, -1) - shifted(0, -1, 1) + shifted(0, -1, -1)
    m_xx, m_yy, m_zz, m_xy, m_xz, m_yz = comps
    return (m_xx * d_xx + m_yy * d_yy + m_zz * d_zz
            + 0.5 * (m_xy * d_xy + m_xz * d_xz + m_yz * d_yz))


def reference(waves_now, waves_prev, epsilon, tilt, azimuth, courant, lag_offsets, table_index, lag_tables):
    comps = tensor(epsilon, tilt, azimuth, courant)
    current, former = waves_now, waves_prev
    for step in range(STEPS):
        extended = jnp.pad(current, ((0, 0), (1, 1), (0, 0), (0, 0)))
        following = 2.0 * current - former + laplace(extended, comps)
        former, current = current, following
    cells_x = current.shape[1]
    cells_y = current.shape[2]
    snap = current.reshape(2, cells_x // 2, 2, cells_y // 2, 2, NZ).sum(axis=(2, 4)) * 0.25
    padded = jnp.pad(snap, ((0, 0), (LAG_REACH, LAG_REACH), (0, 0), (0, 0)))
    half_x = cells_x // 2
    weights = lag_tables[table_index].astype(jnp.float32)

    def one_row(row):
        source = lax.dynamic_index_in_dim(padded[0], row, 1, keepdims=False)
        receiver = lax.dynamic_index_in_dim(padded[1], row, 1, keepdims=False)

        def one_lag(offset):
            left = lax.dynamic_slice_in_dim(source, (LAG_REACH - offset).astype(jnp.int32), half_x, 0)
            right = lax.dynamic_slice_in_dim(receiver, (LAG_REACH + offset).astype(jnp.int32), half_x, 0)
            return left * right

        lagged = jax.vmap(one_lag)(lag_offsets).astype(jnp.bfloat16)
        result = jnp.einsum('zah,hxz->azx', weights, lagged.astype(jnp.float32))
        return result.astype(jnp.bfloat16)

    rows = lax.map(one_row, jnp.arange(cells_y // 2, dtype=jnp.int32))
    return jnp.transpose(rows, (1, 0, 2, 3)).reshape(ANGLES, (cells_y // 2) * NZ, half_x)
```

```python
import functools
import jax
import jax.numpy as jnp
from jax import lax
from jax.experimental import pallas as pl
from jax.experimental.pallas import tpu as pltpu
from jax.sharding import PartitionSpec as P

STEPS = 4
LAG_REACH = 16
PAD = 8
F32 = jnp.float32
SEND = jnp.float32


def sin_cos(x):
    h = x * 0.5
    h2 = h * h
    s = h2 * (-1.0 / 39916800.0) + (1.0 / 362880.0)
    s = s * h2 + (-1.0 / 5040.0)
    s = s * h2 + (1.0 / 120.0)
    s = s * h2 + (-1.0 / 6.0)
    s = s * h2 * h + h
    c = h2 * (1.0 / 479001600.0) + (-1.0 / 3628800.0)
    c = c * h2 + (1.0 / 40320.0)
    c = c * h2 + (-1.0 / 720.0)
    c = c * h2 + (1.0 / 24.0)
    c = c * h2 + (-0.5)
    c = c * h2 + 1.0
    s2 = s + s
    return s2 * c, 1.0 - s2 * s


def wave_kernel(
    n, jr, cols_per, now_hbm, prev_hbm, eps_hbm, tilt_hbm, azi_hbm, cou_hbm, cols_ref,
    buf0, buf1, dz, sz, dy, eps, tilt, azi, cou, coef, pair, snap, sendbuf, halo,
    in_sems, hs_sems, hr_sems, as_sems, ar_sems,
):
    width = eps.shape[0]
    ny = eps.shape[1]
    nz = eps.shape[2]
    rows = pl.ds(PAD, ny)
    up_rows = pl.ds(PAD + 1, ny)
    dn_rows = pl.ds(PAD - 1, ny)
    me = lax.axis_index("gx")
    has_low = me > 0
    has_high = me < n - 1
    bufs = (buf0, buf1)

    copies = [
        pltpu.make_async_copy(tilt_hbm, tilt, in_sems.at[0]),
        pltpu.make_async_copy(azi_hbm, azi, in_sems.at[1]),
        pltpu.make_async_copy(eps_hbm, eps, in_sems.at[2]),
        pltpu.make_async_copy(cou_hbm, cou, in_sems.at[3]),
        pltpu.make_async_copy(now_hbm, buf0.at[:, pl.ds(1, width), rows, :], in_sems.at[4]),
        pltpu.make_async_copy(prev_hbm, buf1.at[:, pl.ds(1, width), rows, :], in_sems.at[5]),
    ]
    for copy in copies:
        copy.start()

    barrier = pltpu.get_barrier_semaphore()

    def greet(k, carry):
        pl.semaphore_signal(
            barrier, inc=1, device_id={"gx": lax.rem(me + k, n)},
            device_id_type=pl.DeviceIdType.MESH,
        )
        return carry

    lax.fori_loop(1, n, greet, 0)

    zero_rows = jnp.zeros((2, width + 2, PAD, nz), F32)
    for ref in (buf0, buf1, dz):
        ref[:, :, pl.ds(0, PAD), :] = zero_rows
        ref[:, :, pl.ds(PAD + ny, PAD), :] = zero_rows
    zero_plane = jnp.zeros((2, ny, nz), F32)
    for ref in (buf0, buf1, dz, dy):
        for plane in (0, width + 1):
            ref[:, plane, rows, :] = zero_plane

    pl.semaphore_wait(barrier, n - 1)

    def halo_copy(step, side):
        if step == 0:
            src = now_hbm.at[:, 0 if side == 0 else width - 1]
        else:
            src = sendbuf.at[step - 1, side]
        return pltpu.make_async_remote_copy(
            src_ref=src,
            dst_ref=halo.at[step, 1 - side],
            send_sem=hs_sems.at[step, side],
            recv_sem=hr_sems.at[step, 1 - side],
            device_id={"gx": me - 1 if side == 0 else me + 1},
            device_id_type=pl.DeviceIdType.MESH,
        )

    def halo_arrived(step, side):
        return pltpu.make_async_remote_copy(
            src_ref=sendbuf.at[0, side],
            dst_ref=halo.at[step, side],
            send_sem=hs_sems.at[step, side],
            recv_sem=hr_sems.at[step, side],
            device_id={"gx": me - 1 if side == 0 else me + 1},
            device_id_type=pl.DeviceIdType.MESH,
        )

    def send_halo(step):
        @pl.when(has_low)
        def _():
            halo_copy(step, 0).start()

        @pl.when(has_high)
        def _():
            halo_copy(step, 1).start()

    send_halo(0)

    for copy in copies[:4]:
        copy.wait()

    def make_coef(x, carry):
        theta_s, theta_c = sin_cos(tilt[x].astype(F32))
        alpha_s, alpha_c = sin_cos(azi[x].astype(F32))
        speed = cou[x].astype(F32)
        e2 = eps[x].astype(F32) * 2.0
        scaled = speed * e2
        base = speed + scaled
        nx = theta_s * alpha_c
        nyy = theta_s * alpha_s
        sx = scaled * nx
        sy = scaled * nyy
        scz = scaled * theta_c
        mxx = base - sx * nx
        myy = base - sy * nyy
        mzz = base - scz * theta_c
        coef[0, x] = mxx
        coef[1, x] = myy
        coef[2, x] = mzz
        coef[3, x] = -0.5 * (sx * nyy)
        coef[4, x] = -0.5 * (scz * nx)
        coef[5, x] = -0.5 * (scz * nyy)
        coef[6, x] = 2.0 - 2.0 * (mxx + myy + mzz)
        return carry

    lax.fori_loop(0, width, make_coef, 0)
    for copy in copies[4:]:
        copy.wait()

    lane = lax.broadcasted_iota(jnp.int32, (ny, nz), 1)
    first = lane == 0
    last = lane == nz - 1

    def z_values(p):
        up = jnp.where(last, 0.0, pltpu.roll(p, nz - 1, axis=1))
        dn = jnp.where(first, 0.0, pltpu.roll(p, 1, axis=1))
        return up - dn, up + dn

    def z_pass(now, x):
        for f in range(2):
            d, s = z_values(now[f, x, rows, :])
            diff = now[f, x, up_rows, :] - now[f, x, dn_rows, :]
            dz[f, x, rows, :] = d
            sz[f, x] = s
            dy[f, x, rows, :] = diff

    def update(now, prv, x):
        c = [coef[k, x - 1] for k in range(7)]
        out = []
        for f in range(2):
            acc = c[6] * now[f, x, rows, :] - prv[f, x, rows, :]
            acc += c[0] * (now[f, x + 1, rows, :] + now[f, x - 1, rows, :])
            acc += c[1] * (now[f, x, up_rows, :] + now[f, x, dn_rows, :])
            acc += c[2] * sz[f, x]
            acc += c[3] * (dy[f, x + 1, rows, :] - dy[f, x - 1, rows, :])
            acc += c[4] * (dz[f, x + 1, rows, :] - dz[f, x - 1, rows, :])
            acc += c[5] * (dz[f, x, up_rows, :] - dz[f, x, dn_rows, :])
            out.append(acc)
        for f in range(2):
            prv[f, x, rows, :] = out[f]
        return out

    for step in range(STEPS):
        now, prv = bufs[step % 2], bufs[(step + 1) % 2]
        z_pass(now, 1)
        z_pass(now, 2)
        z_pass(now, 3)

        def interior(x, carry, now=now, prv=prv):
            update(now, prv, x)
            z_pass(now, x + 2)
            return carry

        lax.fori_loop(2, width - 1, interior, 0)
        update(now, prv, width - 1)

        for side, plane, edge, has in (
            (0, 0, 1, has_low), (1, width + 1, width, has_high),
        ):
            @pl.when(has)
            def _(side=side, plane=plane, now=now, step=step):
                halo_arrived(step, side).wait_recv()
                for f in range(2):
                    p = halo[step, side, f]
                    now[f, plane, rows, :] = p
                    d, _ = z_values(p)
                    dz[f, plane, rows, :] = d
                for f in range(2):
                    dy[f, plane, rows, :] = now[f, plane, up_rows, :] - now[f, plane, dn_rows, :]

            out = update(now, prv, edge)
            if step < STEPS - 1:
                for f in range(2):
                    sendbuf[step, side, f] = out[f]

                @pl.when(has)
                def _(side=side, step=step):
                    halo_copy(step + 1, side).start()

    final = bufs[STEPS % 2]
    half = width // 2

    def make_snap(i, carry):
        for f in range(2):
            pair[f] = final[f, 2 * i + 1, rows, :] + final[f, 2 * i + 2, rows, :]
        for f in range(2):
            even = pair[f, pl.ds(0, ny // 2, stride=2), :]
            odd = pair[f, pl.ds(1, ny // 2, stride=2), :]
            snap[f, pl.ds(i, ny // 2, stride=half), :] = (even + odd) * 0.25
        return carry

    lax.fori_loop(0, half, make_snap, 0)

    span = jr * half

    def piece(target, source):
        start = pl.multiple_of(((target * cols_per) // nz) * half, half)
        return pltpu.make_async_remote_copy(
            src_ref=snap.at[:, pl.ds(start, span), :],
            dst_ref=cols_ref.at[source],
            send_sem=as_sems.at[target],
            recv_sem=ar_sems.at[source],
            device_id={"gx": target},
            device_id_type=pl.DeviceIdType.MESH,
        )

    def send_piece(k, carry):
        piece(lax.rem(me + k, n), me).start()
        return carry

    lax.fori_loop(1, n, send_piece, 0)
    start = pl.multiple_of(((me * cols_per) // nz) * half, half)
    own = pltpu.make_async_copy(snap.at[:, pl.ds(start, span), :], cols_ref.at[me], in_sems.at[6])
    own.start()

    for step in range(STEPS):
        @pl.when(has_low)
        def _(step=step):
            halo_copy(step, 0).wait_send()

        @pl.when(has_high)
        def _(step=step):
            halo_copy(step, 1).wait_send()

    def wait_piece(k, carry):
        piece(lax.rem(me + k, n), me).wait_send()
        piece(lax.rem(me + k, n), lax.rem(me + k, n)).wait_recv()
        return carry

    lax.fori_loop(1, n, wait_piece, 0)
    own.wait()


def image_kernel(
    cols_per, jr, offsets, tables_at, cols_ref, tab_ref, out_ref, lines, wide, prods
):
    n = cols_ref.shape[0]
    half = cols_ref.shape[2] // jr
    nz = cols_ref.shape[3]
    full = n * half
    step = pl.program_id(0)
    tables = tab_ref.shape[0]
    angles = tab_ref.shape[1]
    lags = tab_ref.shape[2]

    @pl.when(step == 0)
    def _():
        for f in range(2):
            for j in range(jr):
                for t in range(full // nz):
                    per = nz // half
                    block = cols_ref[pl.ds(t * per, per), f, pl.ds(j * half, half), :]
                    block = block.reshape(nz, nz).astype(F32)
                    lines[f, j, :, pl.ds(t * nz, nz)] = block.T
        lag = lax.broadcasted_iota(jnp.int32, (lags, lags * 8), 0)
        col = lax.broadcasted_iota(jnp.int32, (lags, lags * 8), 1)
        spread = jnp.where(col // 8 == lag, 1.0, 0.0).astype(jnp.bfloat16)
        flat = tab_ref[...].reshape(tables * angles, lags)
        wide[...] = jnp.dot(flat, spread, preferred_element_type=F32).astype(jnp.bfloat16)

    me = lax.axis_index("gx")
    z0 = lax.rem(me * cols_per, nz)
    x_of = lax.broadcasted_iota(jnp.int32, (8, full), 1)
    ta = tables * angles
    sub = lax.broadcasted_iota(jnp.int32, (8, ta), 0)
    row_c = lax.rem(lax.broadcasted_iota(jnp.int32, (angles * 8, lags * 8), 0), 8)
    col_c = lax.rem(lax.broadcasted_iota(jnp.int32, (angles * 8, lags * 8), 1), 8)
    diagonal = row_c == col_c
    lane_ta = lax.broadcasted_iota(jnp.int32, (angles, 8, ta), 2)
    row_a = lax.broadcasted_iota(jnp.int32, (angles, 8, ta), 0)
    weights = []
    for q in range(2):
        row0 = z0 + step * 16 + q * 8
        chosen = jnp.zeros((8, ta), jnp.int32)
        for c in range(8):
            chosen = jnp.where(sub == c, tables_at[row0 + c], chosen)
        wanted = (chosen * angles)[None] + row_a
        pick = jnp.where(lane_ta == wanted, 1.0, 0.0).reshape(angles * 8, ta)
        dense = jnp.dot(pick.astype(jnp.bfloat16), wide[...], preferred_element_type=F32)
        weights.append(jnp.where(diagonal, dense, 0.0).astype(jnp.bfloat16))

    for j in range(jr):
        results = []
        for q in range(2):
            row0 = pl.multiple_of(z0 + step * 16 + q * 8, 8)
            source = lines[0, j, pl.ds(row0, 8), :]
            receiver = lines[1, j, pl.ds(row0, 8), :]
            slot = j * 2 + q
            for d in range(-LAG_REACH, LAG_REACH):
                reach = abs(d)
                inside = (x_of >= reach) & (x_of < full - reach)
                left = pltpu.roll(source, d % full, axis=1) if d else source
                right = pltpu.roll(receiver, (-d) % full, axis=1) if d else receiver
                product = left * right
                prods[slot, d + LAG_REACH] = jnp.where(inside, product, 0.0) if d else product
            lagged = jnp.concatenate(
                [prods[slot, offsets[h] + LAG_REACH] for h in range(lags)], axis=0
            ).astype(jnp.bfloat16)
            total = jnp.dot(weights[q], lagged, preferred_element_type=F32)
            results.append(total.reshape(angles, 8, full))
        both = jnp.concatenate(results, axis=1)
        out_ref[:, j] = both.astype(jnp.bfloat16)


def local(
    waves_now, waves_prev, epsilon, tilt, azimuth, courant, lag_offsets, table_index, lag_tables
):
    n = lax.axis_size("gx")
    width, ny, nz = epsilon.shape
    half = width // 2
    columns = (ny // 2) * nz
    cols_per = columns // n
    jr = max(1, cols_per // nz)
    full = n * half
    plane = (2, width + 2, ny + 2 * PAD, nz)
    dma = pltpu.SemaphoreType.DMA
    cols = pl.pallas_call(
        functools.partial(wave_kernel, n, jr, cols_per),
        out_shape=jax.ShapeDtypeStruct((n, 2, jr * half, nz), SEND),
        in_specs=[pl.BlockSpec(memory_space=pl.ANY)] * 6,
        out_specs=pl.BlockSpec(memory_space=pltpu.VMEM),
        scratch_shapes=[
            pltpu.VMEM(plane, F32),
            pltpu.VMEM(plane, F32),
            pltpu.VMEM(plane, F32),
            pltpu.VMEM((2, width + 2, ny, nz), F32),
            pltpu.VMEM(plane, F32),
            pltpu.VMEM((width, ny, nz), epsilon.dtype),
            pltpu.VMEM((width, ny, nz), tilt.dtype),
            pltpu.VMEM((width, ny, nz), azimuth.dtype),
            pltpu.VMEM((width, ny, nz), courant.dtype),
            pltpu.VMEM((7, width, ny, nz), F32),
            pltpu.VMEM((2, ny, nz), F32),
            pltpu.VMEM((2, (ny // 2) * half, nz), SEND),
            pltpu.VMEM((STEPS - 1, 2, 2, ny, nz), F32),
            pltpu.VMEM((STEPS, 2, 2, ny, nz), F32),
            dma((7,)),
            dma((STEPS, 2)),
            dma((STEPS, 2)),
            dma((n,)),
            dma((n,)),
        ],
        compiler_params=pltpu.CompilerParams(collective_id=0, has_side_effects=True),
        name="waves",
    )(waves_now, waves_prev, epsilon, tilt, azimuth, courant)

    angles, lags = lag_tables.shape[1:]
    tables = lag_tables.shape[0]
    cz = min(cols_per, nz)
    image = pl.pallas_call(
        functools.partial(image_kernel, cols_per, jr),
        grid=(cz // 16,),
        out_shape=jax.ShapeDtypeStruct((angles, jr, cz, full), jnp.bfloat16),
        in_specs=[
            pl.BlockSpec(memory_space=pltpu.SMEM),
            pl.BlockSpec(memory_space=pltpu.SMEM),
            pl.BlockSpec(memory_space=pltpu.VMEM),
            pl.BlockSpec(memory_space=pltpu.VMEM),
        ],
        out_specs=pl.BlockSpec((angles, jr, 16, full), lambda g: (0, 0, g, 0)),
        scratch_shapes=[
            pltpu.VMEM((2, jr, nz, full), F32),
            pltpu.VMEM((tables * angles, lags * 8), jnp.bfloat16),
            pltpu.VMEM((jr * 2, 2 * LAG_REACH, 8, full), F32),
        ],
        name="image",
    )(lag_offsets, table_index, cols, lag_tables)
    return image.reshape(angles, cols_per, full)


def solution(mesh):
    wave = P(None, ("shot", "gx"), None, None)
    cell = P("gx", None, None)
    return jax.shard_map(
        local,
        mesh=mesh,
        in_specs=(wave, wave, cell, cell, cell, cell, P(), P(), P()),
        out_specs=P(None, ("shot", "gx"), None),
        check_vma=False,
    )
```

```python
import functools
import jax
import jax.numpy as jnp
from jax import lax
from jax.experimental import pallas as pl
from jax.experimental.pallas import tpu as pltpu
from jax.sharding import PartitionSpec as P

STEPS = 4
LAG_REACH = 16
PAD = 8
F32 = jnp.float32
SEND = jnp.bfloat16


def sin_cos(x):
    h = x * 0.5
    h2 = h * h
    s = h2 * 2.609020676498479e-06 + (-0.00019811149207883466)
    s = s * h2 + 0.008333088613525165
    s = s * h2 + (-0.16666660477455342)
    s = s * h2 * h + h
    c = h2 * (-2.607799327383753e-07) + 2.4761934264809493e-05
    c = c * h2 + (-0.0013888404392126607)
    c = c * h2 + 0.04166664079116777
    c = c * h2 + (-0.4999999955092854)
    c = c * h2 + 1.0
    s2 = s + s
    return s2 * c, 1.0 - s2 * s


def wave_kernel(
    n, jr, cols_per, now_hbm, prev_hbm, eps_hbm, tilt_hbm, azi_hbm, cou_hbm, cols_ref,
    buf0, buf1, dz, dy, eps, tilt, azi, cou, coef, pair, snap, snap_send, sendbuf, halo,
    in_sems, hs_sems, hr_sems, as_sems, ar_sems,
):
    width = eps.shape[0]
    ny = eps.shape[1]
    nz = eps.shape[2]
    rows = pl.ds(PAD, ny)
    up_rows = pl.ds(PAD + 1, ny)
    dn_rows = pl.ds(PAD - 1, ny)
    me = lax.axis_index("gx")
    has_low = me > 0
    has_high = me < n - 1
    bufs = (buf0, buf1)

    copies = [
        pltpu.make_async_copy(tilt_hbm, tilt, in_sems.at[0]),
        pltpu.make_async_copy(azi_hbm, azi, in_sems.at[1]),
        pltpu.make_async_copy(eps_hbm, eps, in_sems.at[2]),
        pltpu.make_async_copy(cou_hbm, cou, in_sems.at[3]),
        pltpu.make_async_copy(now_hbm, buf0.at[:, pl.ds(1, width), rows, :], in_sems.at[4]),
        pltpu.make_async_copy(prev_hbm, buf1.at[:, pl.ds(1, width), rows, :], in_sems.at[5]),
    ]
    for copy in copies:
        copy.start()

    barrier = pltpu.get_barrier_semaphore()

    def greet(k, carry):
        pl.semaphore_signal(
            barrier, inc=1, device_id={"gx": lax.rem(me + k, n)},
            device_id_type=pl.DeviceIdType.MESH,
        )
        return carry

    lax.fori_loop(1, n, greet, 0)

    zero_rows = jnp.zeros((2, width + 2, PAD, nz), F32)
    for ref in (buf0, buf1):
        ref[:, :, pl.ds(0, PAD), :] = zero_rows
        ref[:, :, pl.ds(PAD + ny, PAD), :] = zero_rows
    zero_plane = jnp.zeros((2, ny, nz), F32)
    for plane in (0, width + 1):
        for ref in (buf0, buf1):
            ref[:, plane, rows, :] = zero_plane
        for ref in (dz, dy):
            ref[:, plane] = zero_plane

    pl.semaphore_wait(barrier, n - 1)

    def halo_copy(step, side):
        if step == 0:
            src = now_hbm.at[:, 0 if side == 0 else width - 1]
        else:
            src = sendbuf.at[step - 1, side]
        return pltpu.make_async_remote_copy(
            src_ref=src,
            dst_ref=halo.at[step, 1 - side],
            send_sem=hs_sems.at[step, side],
            recv_sem=hr_sems.at[step, 1 - side],
            device_id={"gx": me - 1 if side == 0 else me + 1},
            device_id_type=pl.DeviceIdType.MESH,
        )

    def halo_arrived(step, side):
        return pltpu.make_async_remote_copy(
            src_ref=sendbuf.at[0, side],
            dst_ref=halo.at[step, side],
            send_sem=hs_sems.at[step, side],
            recv_sem=hr_sems.at[step, side],
            device_id={"gx": me - 1 if side == 0 else me + 1},
            device_id_type=pl.DeviceIdType.MESH,
        )

    def send_halo(step):
        @pl.when(has_low)
        def _():
            halo_copy(step, 0).start()

        @pl.when(has_high)
        def _():
            halo_copy(step, 1).start()

    send_halo(0)

    for copy in copies[:4]:
        copy.wait()

    def make_coef(x, carry):
        theta_s, theta_c = sin_cos(tilt[x].astype(F32))
        alpha_s, alpha_c = sin_cos(azi[x].astype(F32))
        speed = cou[x].astype(F32)
        e2 = eps[x].astype(F32) * 2.0
        scaled = speed * e2
        base = speed + scaled
        nx = theta_s * alpha_c
        nyy = theta_s * alpha_s
        sx = scaled * nx
        sy = scaled * nyy
        scz = scaled * theta_c
        mxx = base - sx * nx
        myy = base - sy * nyy
        mzz = base - scz * theta_c
        coef[0, x] = mxx
        coef[1, x] = myy
        coef[2, x] = mzz
        coef[3, x] = -0.5 * (sx * nyy)
        coef[4, x] = -0.5 * (scz * nx)
        coef[5, x] = -0.5 * (scz * nyy)
        coef[6, x] = 2.0 - 2.0 * (mxx + myy + mzz)
        return carry

    lax.fori_loop(0, width, make_coef, 0)
    for copy in copies[4:]:
        copy.wait()

    chunk = 16
    starts = range(0, ny, chunk)

    def z_shifts(p):
        lane = lax.broadcasted_iota(jnp.int32, p.shape, 1)
        up = jnp.where(lane == nz - 1, 0.0, pltpu.roll(p, nz - 1, axis=1))
        dn = jnp.where(lane == 0, 0.0, pltpu.roll(p, 1, axis=1))
        return up, dn

    def own_plane(now, prv, x):
        for y in starts:
            here = pl.ds(y, chunk)
            c1, c2, c5, c6 = [coef[k, x - 1, here, :] for k in (1, 2, 5, 6)]
            for f in range(2):
                p = now[f, x, pl.ds(PAD + y, chunk), :]
                pu = now[f, x, pl.ds(PAD + y + 1, chunk), :]
                pd = now[f, x, pl.ds(PAD + y - 1, chunk), :]
                before = prv[f, x, pl.ds(PAD + y, chunk), :]
                up, dn = z_shifts(p)
                diff = pu - pd
                yup, ydn = z_shifts(diff)
                part = c6 * p - before + c1 * (pu + pd)
                part = part + (c2 * (up + dn) + c5 * (yup - ydn))
                prv[f, x, pl.ds(PAD + y, chunk), :] = part
                dz[f, x, here, :] = up - dn
                dy[f, x, here, :] = diff

    def update(now, prv, x):
        for y in starts:
            here = pl.ds(y, chunk)
            mid = pl.ds(PAD + y, chunk)
            c0, c3, c4 = [coef[k, x - 1, here, :] for k in (0, 3, 4)]
            for f in range(2):
                acc = prv[f, x, mid, :] + c0 * (now[f, x + 1, mid, :] + now[f, x - 1, mid, :])
                acc += c3 * (dy[f, x + 1, here, :] - dy[f, x - 1, here, :])
                acc += c4 * (dz[f, x + 1, here, :] - dz[f, x - 1, here, :])
                prv[f, x, mid, :] = acc

    for step in range(STEPS):
        now, prv = bufs[step % 2], bufs[(step + 1) % 2]
        for x in (1, 2, 3):
            own_plane(now, prv, x)

        def interior(x, carry, now=now, prv=prv):
            update(now, prv, x)
            own_plane(now, prv, x + 2)
            return carry

        lax.fori_loop(2, width - 1, interior, 0)
        update(now, prv, width - 1)

        for side, plane, edge, has in (
            (0, 0, 1, has_low), (1, width + 1, width, has_high),
        ):
            @pl.when(has)
            def _(side=side, plane=plane, now=now, step=step):
                halo_arrived(step, side).wait_recv()
                for f in range(2):
                    p = halo[step, side, f]
                    now[f, plane, rows, :] = p
                    up, dn = z_shifts(p)
                    dz[f, plane] = up - dn
                for f in range(2):
                    dy[f, plane] = now[f, plane, up_rows, :] - now[f, plane, dn_rows, :]

            update(now, prv, edge)
            if step < STEPS - 1:
                for f in range(2):
                    sendbuf[step, side, f] = prv[f, edge, rows, :]

                @pl.when(has)
                def _(side=side, step=step):
                    halo_copy(step + 1, side).start()

    final = bufs[STEPS % 2]
    half = width // 2

    def make_snap(i, carry):
        for f in range(2):
            pair[f] = final[f, 2 * i + 1, rows, :] + final[f, 2 * i + 2, rows, :]
        for f in range(2):
            even = pair[f, pl.ds(0, ny // 2, stride=2), :]
            odd = pair[f, pl.ds(1, ny // 2, stride=2), :]
            snap[f, pl.ds(i, ny // 2, stride=half), :] = (even + odd) * 0.25
        return carry

    lax.fori_loop(0, half, make_snap, 0)

    span = jr * half

    def piece(target, source):
        start = pl.multiple_of(((target * cols_per) // nz) * half, half)
        return pltpu.make_async_remote_copy(
            src_ref=snap_send.at[:, pl.ds(start, span), :],
            dst_ref=cols_ref.at[source],
            send_sem=as_sems.at[target],
            recv_sem=ar_sems.at[source],
            device_id={"gx": target},
            device_id_type=pl.DeviceIdType.MESH,
        )

    snap_send[...] = snap[...].astype(SEND)

    def send_piece(k, carry):
        piece(lax.rem(me + k, n), me).start()
        return carry

    lax.fori_loop(n // 2, n, send_piece, 0)
    lax.fori_loop(1, n // 2, send_piece, 0)
    start = pl.multiple_of(((me * cols_per) // nz) * half, half)
    own = pltpu.make_async_copy(snap_send.at[:, pl.ds(start, span), :], cols_ref.at[me], in_sems.at[6])
    own.start()

    for step in range(STEPS):
        @pl.when(has_low)
        def _(step=step):
            halo_copy(step, 0).wait_send()

        @pl.when(has_high)
        def _(step=step):
            halo_copy(step, 1).wait_send()

    def wait_piece(k, carry):
        piece(lax.rem(me + k, n), me).wait_send()
        piece(lax.rem(me + k, n), lax.rem(me + k, n)).wait_recv()
        return carry

    lax.fori_loop(1, n, wait_piece, 0)
    own.wait()


def image_kernel(
    cols_per, jr, offsets, tables_at, cols_ref, tab_ref, out_ref, lines, wide, prods
):
    n = cols_ref.shape[0]
    half = cols_ref.shape[2] // jr
    nz = cols_ref.shape[3]
    full = n * half
    step = pl.program_id(0)
    tables = tab_ref.shape[0]
    angles = tab_ref.shape[1]
    lags = tab_ref.shape[2]

    @pl.when(step == 0)
    def _():
        for f in range(2):
            for j in range(jr):
                for t in range(full // nz):
                    per = nz // half
                    block = cols_ref[pl.ds(t * per, per), f, pl.ds(j * half, half), :]
                    block = block.reshape(nz, nz).astype(F32)
                    lines[f, j, :, pl.ds(t * nz, nz)] = block.T
        lag = lax.broadcasted_iota(jnp.int32, (lags, lags * 8), 0)
        col = lax.broadcasted_iota(jnp.int32, (lags, lags * 8), 1)
        spread = jnp.where(col // 8 == lag, 1.0, 0.0).astype(jnp.bfloat16)
        flat = tab_ref[...].reshape(tables * angles, lags)
        wide[...] = jnp.dot(flat, spread, preferred_element_type=F32).astype(jnp.bfloat16)

    me = lax.axis_index("gx")
    z0 = lax.rem(me * cols_per, nz)
    lane = lax.broadcasted_iota(jnp.int32, (8, nz), 1)
    tiles = full // nz
    ta = tables * angles
    sub = lax.broadcasted_iota(jnp.int32, (8, ta), 0)
    row_c = lax.rem(lax.broadcasted_iota(jnp.int32, (angles * 8, lags * 8), 0), 8)
    col_c = lax.rem(lax.broadcasted_iota(jnp.int32, (angles * 8, lags * 8), 1), 8)
    diagonal = row_c == col_c
    lane_ta = lax.broadcasted_iota(jnp.int32, (angles, 8, ta), 2)
    row_a = lax.broadcasted_iota(jnp.int32, (angles, 8, ta), 0)
    weights = []
    for q in range(2):
        row0 = z0 + step * 16 + q * 8
        chosen = jnp.zeros((8, ta), jnp.int32)
        for c in range(8):
            chosen = jnp.where(sub == c, tables_at[row0 + c], chosen)
        wanted = (chosen * angles)[None] + row_a
        pick = jnp.where(lane_ta == wanted, 1.0, 0.0).reshape(angles * 8, ta)
        dense = jnp.dot(pick.astype(jnp.bfloat16), wide[...], preferred_element_type=F32)
        weights.append(jnp.where(diagonal, dense, 0.0).astype(jnp.bfloat16))

    def moved(parts, d):
        if d == 0:
            return parts
        turned = [pltpu.roll(part, d % nz, axis=1) for part in parts]
        zero = jnp.zeros((8, nz), F32)
        if d > 0:
            return [
                jnp.where(lane >= d, turned[t], turned[t - 1] if t else zero)
                for t in range(tiles)
            ]
        return [
            jnp.where(lane < nz + d, turned[t], turned[t + 1] if t + 1 < tiles else zero)
            for t in range(tiles)
        ]

    for j in range(jr):
        results = []
        for q in range(2):
            row0 = pl.multiple_of(z0 + step * 16 + q * 8, 8)
            source = [lines[0, j, pl.ds(row0, 8), pl.ds(t * nz, nz)] for t in range(tiles)]
            receiver = [lines[1, j, pl.ds(row0, 8), pl.ds(t * nz, nz)] for t in range(tiles)]
            slot = j * 2 + q
            for d in range(-LAG_REACH, LAG_REACH):
                left, right = moved(source, d), moved(receiver, -d)
                for t in range(tiles):
                    prods[slot, d + LAG_REACH, :, pl.ds(t * nz, nz)] = left[t] * right[t]
            lagged = jnp.concatenate(
                [prods[slot, offsets[h] + LAG_REACH] for h in range(lags)], axis=0
            ).astype(jnp.bfloat16)
            total = jnp.dot(weights[q], lagged, preferred_element_type=F32)
            results.append(total.reshape(angles, 8, full))
        both = jnp.concatenate(results, axis=1)
        out_ref[:, j] = both.astype(jnp.bfloat16)


def local(
    waves_now, waves_prev, epsilon, tilt, azimuth, courant, lag_offsets, table_index, lag_tables
):
    n = lax.axis_size("gx")
    width, ny, nz = epsilon.shape
    half = width // 2
    columns = (ny // 2) * nz
    cols_per = columns // n
    jr = max(1, cols_per // nz)
    full = n * half
    plane = (2, width + 2, ny + 2 * PAD, nz)
    dma = pltpu.SemaphoreType.DMA
    cols = pl.pallas_call(
        functools.partial(wave_kernel, n, jr, cols_per),
        out_shape=jax.ShapeDtypeStruct((n, 2, jr * half, nz), SEND),
        in_specs=[pl.BlockSpec(memory_space=pl.ANY)] * 6,
        out_specs=pl.BlockSpec(memory_space=pltpu.VMEM),
        scratch_shapes=[
            pltpu.VMEM(plane, F32),
            pltpu.VMEM(plane, F32),
            pltpu.VMEM((2, width + 2, ny, nz), F32),
            pltpu.VMEM((2, width + 2, ny, nz), F32),
            pltpu.VMEM((width, ny, nz), epsilon.dtype),
            pltpu.VMEM((width, ny, nz), tilt.dtype),
            pltpu.VMEM((width, ny, nz), azimuth.dtype),
            pltpu.VMEM((width, ny, nz), courant.dtype),
            pltpu.VMEM((7, width, ny, nz), F32),
            pltpu.VMEM((2, ny, nz), F32),
            pltpu.VMEM((2, (ny // 2) * half, nz), F32),
            pltpu.VMEM((2, (ny // 2) * half, nz), SEND),
            pltpu.VMEM((STEPS - 1, 2, 2, ny, nz), F32),
            pltpu.VMEM((STEPS, 2, 2, ny, nz), F32),
            dma((7,)),
            dma((STEPS, 2)),
            dma((STEPS, 2)),
            dma((n,)),
            dma((n,)),
        ],
        compiler_params=pltpu.CompilerParams(collective_id=0, has_side_effects=True),
        name="waves",
    )(waves_now, waves_prev, epsilon, tilt, azimuth, courant)

    angles, lags = lag_tables.shape[1:]
    tables = lag_tables.shape[0]
    cz = min(cols_per, nz)
    image = pl.pallas_call(
        functools.partial(image_kernel, cols_per, jr),
        grid=(cz // 16,),
        out_shape=jax.ShapeDtypeStruct((angles, jr, cz, full), jnp.bfloat16),
        in_specs=[
            pl.BlockSpec(memory_space=pltpu.SMEM),
            pl.BlockSpec(memory_space=pltpu.SMEM),
            pl.BlockSpec(memory_space=pltpu.VMEM),
            pl.BlockSpec(memory_space=pltpu.VMEM),
        ],
        out_specs=pl.BlockSpec((angles, jr, 16, full), lambda g: (0, 0, g, 0)),
        scratch_shapes=[
            pltpu.VMEM((2, jr, nz, full), F32),
            pltpu.VMEM((tables * angles, lags * 8), jnp.bfloat16),
            pltpu.VMEM((jr * 2, 2 * LAG_REACH, 8, full), F32),
        ],
        name="image",
    )(lag_offsets, table_index, cols, lag_tables)
    return image.reshape(angles, cols_per, full)


def solution(mesh):
    wave = P(None, ("shot", "gx"), None, None)
    cell = P("gx", None, None)
    return jax.shard_map(
        local,
        mesh=mesh,
        in_specs=(wave, wave, cell, cell, cell, cell, P(), P(), P()),
        out_specs=P(None, ("shot", "gx"), None),
        check_vma=False,
    )
```

```python
import functools
import jax
import jax.numpy as jnp
from jax import lax
from jax.experimental import pallas as pl
from jax.experimental.pallas import tpu as pltpu
from jax.sharding import PartitionSpec as P

STEPS = 4
LAG_REACH = 16
PAD = 8
F32 = jnp.float32
SEND = jnp.bfloat16


def sin_cos(x):
    h = x * 0.5
    h2 = h * h
    s = h2 * 2.609020676498479e-06 + (-0.00019811149207883466)
    s = s * h2 + 0.008333088613525165
    s = s * h2 + (-0.16666660477455342)
    s = s * h2 * h + h
    c = h2 * (-2.607799327383753e-07) + 2.4761934264809493e-05
    c = c * h2 + (-0.0013888404392126607)
    c = c * h2 + 0.04166664079116777
    c = c * h2 + (-0.4999999955092854)
    c = c * h2 + 1.0
    s2 = s + s
    return s2 * c, 1.0 - s2 * s


def wave_kernel(
    n, jr, cols_per, now_hbm, prev_hbm, eps_hbm, tilt_hbm, azi_hbm, cou_hbm, cols_ref,
    buf0, buf1, dz, dy, part, eps, tilt, azi, cou, coef, pair, snap, snap_send, sendbuf, halo,
    in_sems, hs_sems, hr_sems, as_sems, ar_sems,
):
    width = eps.shape[0]
    ny = eps.shape[1]
    nz = eps.shape[2]
    rows = pl.ds(PAD, ny)
    up_rows = pl.ds(PAD + 1, ny)
    dn_rows = pl.ds(PAD - 1, ny)
    me = lax.axis_index("gx")
    has_low = me > 0
    has_high = me < n - 1
    bufs = (buf0, buf1)

    copies = [
        pltpu.make_async_copy(tilt_hbm, tilt, in_sems.at[0]),
        pltpu.make_async_copy(azi_hbm, azi, in_sems.at[1]),
        pltpu.make_async_copy(eps_hbm, eps, in_sems.at[2]),
        pltpu.make_async_copy(cou_hbm, cou, in_sems.at[3]),
        pltpu.make_async_copy(now_hbm, buf0.at[:, pl.ds(1, width), rows, :], in_sems.at[4]),
        pltpu.make_async_copy(prev_hbm, buf1.at[:, pl.ds(1, width), rows, :], in_sems.at[5]),
    ]
    for copy in copies:
        copy.start()

    barrier = pltpu.get_barrier_semaphore()

    def greet(k, carry):
        pl.semaphore_signal(
            barrier, inc=1, device_id={"gx": lax.rem(me + k, n)},
            device_id_type=pl.DeviceIdType.MESH,
        )
        return carry

    lax.fori_loop(1, n, greet, 0)

    zero_rows = jnp.zeros((2, width + 2, PAD, nz), F32)
    for ref in (buf0, buf1, dz):
        ref[:, :, pl.ds(0, PAD), :] = zero_rows
        ref[:, :, pl.ds(PAD + ny, PAD), :] = zero_rows
    zero_plane = jnp.zeros((2, ny, nz), F32)
    for plane in (0, width + 1):
        for ref in (buf0, buf1):
            ref[:, plane, rows, :] = zero_plane
        dz[:, plane, rows, :] = zero_plane
        dy[:, plane] = zero_plane

    pl.semaphore_wait(barrier, n - 1)

    def halo_copy(step, side):
        if step == 0:
            src = now_hbm.at[:, 0 if side == 0 else width - 1]
        else:
            src = sendbuf.at[step - 1, side]
        return pltpu.make_async_remote_copy(
            src_ref=src,
            dst_ref=halo.at[step, 1 - side],
            send_sem=hs_sems.at[step, side],
            recv_sem=hr_sems.at[step, 1 - side],
            device_id={"gx": me - 1 if side == 0 else me + 1},
            device_id_type=pl.DeviceIdType.MESH,
        )

    def halo_arrived(step, side):
        return pltpu.make_async_remote_copy(
            src_ref=sendbuf.at[0, side],
            dst_ref=halo.at[step, side],
            send_sem=hs_sems.at[step, side],
            recv_sem=hr_sems.at[step, side],
            device_id={"gx": me - 1 if side == 0 else me + 1},
            device_id_type=pl.DeviceIdType.MESH,
        )

    def send_halo(step):
        @pl.when(has_low)
        def _():
            halo_copy(step, 0).start()

        @pl.when(has_high)
        def _():
            halo_copy(step, 1).start()

    send_halo(0)

    for copy in copies[:4]:
        copy.wait()

    def make_coef(x, carry):
        theta_s, theta_c = sin_cos(tilt[x].astype(F32))
        alpha_s, alpha_c = sin_cos(azi[x].astype(F32))
        speed = cou[x].astype(F32)
        e2 = eps[x].astype(F32) * 2.0
        scaled = speed * e2
        base = speed + scaled
        nx = theta_s * alpha_c
        nyy = theta_s * alpha_s
        sx = scaled * nx
        sy = scaled * nyy
        scz = scaled * theta_c
        mxx = base - sx * nx
        myy = base - sy * nyy
        mzz = base - scz * theta_c
        coef[0, x] = mxx
        coef[1, x] = myy
        coef[2, x] = mzz
        coef[3, x] = -0.5 * (sx * nyy)
        coef[4, x] = -0.5 * (scz * nx)
        coef[5, x] = -0.5 * (scz * nyy)
        coef[6, x] = 2.0 - 2.0 * (mxx + myy + mzz)
        return carry

    lax.fori_loop(0, width, make_coef, 0)
    for copy in copies[4:]:
        copy.wait()

    chunk = 16
    starts = range(0, ny, chunk)

    def z_shifts(p):
        lane = lax.broadcasted_iota(jnp.int32, p.shape, 1)
        up = jnp.where(lane == nz - 1, 0.0, pltpu.roll(p, nz - 1, axis=1))
        dn = jnp.where(lane == 0, 0.0, pltpu.roll(p, 1, axis=1))
        return up, dn

    def turns(now, x, y):
        return [z_shifts(now[f, x, pl.ds(PAD + y, chunk), :]) for f in range(2)]

    def own_rows(now, x, y, turned):
        here = pl.ds(y, chunk)
        c1, c2, c6 = [coef[k, x - 1, here, :] for k in (1, 2, 6)]
        for f in range(2):
            p = now[f, x, pl.ds(PAD + y, chunk), :]
            pu = now[f, x, pl.ds(PAD + y + 1, chunk), :]
            pd = now[f, x, pl.ds(PAD + y - 1, chunk), :]
            up, dn = turned[f]
            part[f, x, here, :] = c6 * p + c1 * (pu + pd) + c2 * (up + dn)
            dz[f, x, pl.ds(PAD + y, chunk), :] = up - dn
            dy[f, x, here, :] = pu - pd

    def own_plane(now, x):
        for y in starts:
            own_rows(now, x, y, turns(now, x, y))

    def update(now, prv, x, picked=starts):
        for y in picked:
            here = pl.ds(y, chunk)
            mid = pl.ds(PAD + y, chunk)
            c0, c3, c4, c5 = [coef[k, x - 1, here, :] for k in (0, 3, 4, 5)]
            for f in range(2):
                acc = part[f, x, here, :] - prv[f, x, mid, :]
                acc += c0 * (now[f, x + 1, mid, :] + now[f, x - 1, mid, :])
                acc += c3 * (dy[f, x + 1, here, :] - dy[f, x - 1, here, :])
                acc += c4 * (dz[f, x + 1, mid, :] - dz[f, x - 1, mid, :])
                acc += c5 * (
                    dz[f, x, pl.ds(PAD + y + 1, chunk), :] - dz[f, x, pl.ds(PAD + y - 1, chunk), :]
                )
                prv[f, x, mid, :] = acc

    for step in range(STEPS):
        now, prv = bufs[step % 2], bufs[(step + 1) % 2]
        for x in (1, 2, 3):
            own_plane(now, x)

        def interior(x, carry, now=now, prv=prv):
            turned = turns(now, x + 2, 0)
            for y in starts:
                update(now, prv, x, (y,))
                ahead = turns(now, x + 2, y + chunk) if y + chunk < ny else None
                own_rows(now, x + 2, y, turned)
                turned = ahead
            return carry

        lax.fori_loop(2, width - 1, interior, 0)
        update(now, prv, width - 1)

        for side, plane, edge, has in (
            (0, 0, 1, has_low), (1, width + 1, width, has_high),
        ):
            @pl.when(has)
            def _(side=side, plane=plane, now=now, step=step):
                halo_arrived(step, side).wait_recv()
                for f in range(2):
                    p = halo[step, side, f]
                    now[f, plane, rows, :] = p
                    up, dn = z_shifts(p)
                    dz[f, plane, rows, :] = up - dn
                for f in range(2):
                    dy[f, plane] = now[f, plane, up_rows, :] - now[f, plane, dn_rows, :]

            update(now, prv, edge)
            if step < STEPS - 1:
                for f in range(2):
                    sendbuf[step, side, f] = prv[f, edge, rows, :]

                @pl.when(has)
                def _(side=side, step=step):
                    halo_copy(step + 1, side).start()

    final = bufs[STEPS % 2]
    half = width // 2

    def make_snap(i, carry):
        for f in range(2):
            pair[f] = final[f, 2 * i + 1, rows, :] + final[f, 2 * i + 2, rows, :]
        for f in range(2):
            even = pair[f, pl.ds(0, ny // 2, stride=2), :]
            odd = pair[f, pl.ds(1, ny // 2, stride=2), :]
            snap[f, pl.ds(i, ny // 2, stride=half), :] = (even + odd) * 0.25
        return carry

    lax.fori_loop(0, half, make_snap, 0)

    span = jr * half

    def piece(target, source):
        start = pl.multiple_of(((target * cols_per) // nz) * half, half)
        return pltpu.make_async_remote_copy(
            src_ref=snap_send.at[:, pl.ds(start, span), :],
            dst_ref=cols_ref.at[source],
            send_sem=as_sems.at[target],
            recv_sem=ar_sems.at[source],
            device_id={"gx": target},
            device_id_type=pl.DeviceIdType.MESH,
        )

    snap_send[...] = snap[...].astype(SEND)

    def send_piece(k, carry):
        piece(lax.rem(me + k, n), me).start()
        return carry

    lax.fori_loop(n // 2, n, send_piece, 0)
    lax.fori_loop(1, n // 2, send_piece, 0)
    start = pl.multiple_of(((me * cols_per) // nz) * half, half)
    own = pltpu.make_async_copy(snap_send.at[:, pl.ds(start, span), :], cols_ref.at[me], in_sems.at[6])
    own.start()

    for step in range(STEPS):
        @pl.when(has_low)
        def _(step=step):
            halo_copy(step, 0).wait_send()

        @pl.when(has_high)
        def _(step=step):
            halo_copy(step, 1).wait_send()

    def wait_piece(k, carry):
        piece(lax.rem(me + k, n), me).wait_send()
        piece(lax.rem(me + k, n), lax.rem(me + k, n)).wait_recv()
        return carry

    lax.fori_loop(1, n, wait_piece, 0)
    own.wait()


def image_kernel(
    cols_per, jr, offsets, tables_at, cols_ref, tab_ref, out_ref, lines, wide, prods
):
    n = cols_ref.shape[0]
    half = cols_ref.shape[2] // jr
    nz = cols_ref.shape[3]
    full = n * half
    step = pl.program_id(0)
    tables = tab_ref.shape[0]
    angles = tab_ref.shape[1]
    lags = tab_ref.shape[2]

    @pl.when(step == 0)
    def _():
        for f in range(2):
            for j in range(jr):
                for t in range(full // nz):
                    per = nz // half
                    block = cols_ref[pl.ds(t * per, per), f, pl.ds(j * half, half), :]
                    block = block.reshape(nz, nz).astype(F32)
                    lines[f, j, :, pl.ds(t * nz, nz)] = block.T
        lag = lax.broadcasted_iota(jnp.int32, (lags, lags * 8), 0)
        col = lax.broadcasted_iota(jnp.int32, (lags, lags * 8), 1)
        spread = jnp.where(col // 8 == lag, 1.0, 0.0).astype(jnp.bfloat16)
        flat = tab_ref[...].reshape(tables * angles, lags)
        wide[...] = jnp.dot(flat, spread, preferred_element_type=F32).astype(jnp.bfloat16)

    me = lax.axis_index("gx")
    z0 = lax.rem(me * cols_per, nz)
    lane = lax.broadcasted_iota(jnp.int32, (8, nz), 1)
    tiles = full // nz
    ta = tables * angles
    sub = lax.broadcasted_iota(jnp.int32, (8, ta), 0)
    row_c = lax.rem(lax.broadcasted_iota(jnp.int32, (angles * 8, lags * 8), 0), 8)
    col_c = lax.rem(lax.broadcasted_iota(jnp.int32, (angles * 8, lags * 8), 1), 8)
    diagonal = row_c == col_c
    lane_ta = lax.broadcasted_iota(jnp.int32, (angles, 8, ta), 2)
    row_a = lax.broadcasted_iota(jnp.int32, (angles, 8, ta), 0)
    weights = []
    for q in range(2):
        row0 = z0 + step * 16 + q * 8
        chosen = jnp.zeros((8, ta), jnp.int32)
        for c in range(8):
            chosen = jnp.where(sub == c, tables_at[row0 + c], chosen)
        wanted = (chosen * angles)[None] + row_a
        pick = jnp.where(lane_ta == wanted, 1.0, 0.0).reshape(angles * 8, ta)
        dense = jnp.dot(pick.astype(jnp.bfloat16), wide[...], preferred_element_type=F32)
        weights.append(jnp.where(diagonal, dense, 0.0).astype(jnp.bfloat16))

    def moved(parts, d):
        if d == 0:
            return parts
        turned = [pltpu.roll(part, d % nz, axis=1) for part in parts]
        zero = jnp.zeros((8, nz), F32)
        if d > 0:
            return [
                jnp.where(lane >= d, turned[t], turned[t - 1] if t else zero)
                for t in range(tiles)
            ]
        return [
            jnp.where(lane < nz + d, turned[t], turned[t + 1] if t + 1 < tiles else zero)
            for t in range(tiles)
        ]

    for j in range(jr):
        results = []
        for q in range(2):
            row0 = pl.multiple_of(z0 + step * 16 + q * 8, 8)
            source = [lines[0, j, pl.ds(row0, 8), pl.ds(t * nz, nz)] for t in range(tiles)]
            receiver = [lines[1, j, pl.ds(row0, 8), pl.ds(t * nz, nz)] for t in range(tiles)]
            slot = j * 2 + q
            for d in range(-LAG_REACH, LAG_REACH):
                left, right = moved(source, d), moved(receiver, -d)
                for t in range(tiles):
                    prods[slot, d + LAG_REACH, :, pl.ds(t * nz, nz)] = left[t] * right[t]
            lagged = jnp.concatenate(
                [prods[slot, offsets[h] + LAG_REACH] for h in range(lags)], axis=0
            ).astype(jnp.bfloat16)
            total = jnp.dot(weights[q], lagged, preferred_element_type=F32)
            results.append(total.reshape(angles, 8, full))
        both = jnp.concatenate(results, axis=1)
        out_ref[:, j] = both.astype(jnp.bfloat16)


def local(
    waves_now, waves_prev, epsilon, tilt, azimuth, courant, lag_offsets, table_index, lag_tables
):
    n = lax.axis_size("gx")
    width, ny, nz = epsilon.shape
    half = width // 2
    columns = (ny // 2) * nz
    cols_per = columns // n
    jr = max(1, cols_per // nz)
    full = n * half
    plane = (2, width + 2, ny + 2 * PAD, nz)
    dma = pltpu.SemaphoreType.DMA
    cols = pl.pallas_call(
        functools.partial(wave_kernel, n, jr, cols_per),
        out_shape=jax.ShapeDtypeStruct((n, 2, jr * half, nz), SEND),
        in_specs=[pl.BlockSpec(memory_space=pl.ANY)] * 6,
        out_specs=pl.BlockSpec(memory_space=pltpu.VMEM),
        scratch_shapes=[
            pltpu.VMEM(plane, F32),
            pltpu.VMEM(plane, F32),
            pltpu.VMEM(plane, F32),
            pltpu.VMEM((2, width + 2, ny, nz), F32),
            pltpu.VMEM((2, width + 2, ny, nz), F32),
            pltpu.VMEM((width, ny, nz), epsilon.dtype),
            pltpu.VMEM((width, ny, nz), tilt.dtype),
            pltpu.VMEM((width, ny, nz), azimuth.dtype),
            pltpu.VMEM((width, ny, nz), courant.dtype),
            pltpu.VMEM((7, width, ny, nz), F32),
            pltpu.VMEM((2, ny, nz), F32),
            pltpu.VMEM((2, (ny // 2) * half, nz), F32),
            pltpu.VMEM((2, (ny // 2) * half, nz), SEND),
            pltpu.VMEM((STEPS - 1, 2, 2, ny, nz), F32),
            pltpu.VMEM((STEPS, 2, 2, ny, nz), F32),
            dma((7,)),
            dma((STEPS, 2)),
            dma((STEPS, 2)),
            dma((n,)),
            dma((n,)),
        ],
        compiler_params=pltpu.CompilerParams(collective_id=0, has_side_effects=True),
        name="waves",
    )(waves_now, waves_prev, epsilon, tilt, azimuth, courant)

    angles, lags = lag_tables.shape[1:]
    tables = lag_tables.shape[0]
    cz = min(cols_per, nz)
    image = pl.pallas_call(
        functools.partial(image_kernel, cols_per, jr),
        grid=(cz // 16,),
        out_shape=jax.ShapeDtypeStruct((angles, jr, cz, full), jnp.bfloat16),
        in_specs=[
            pl.BlockSpec(memory_space=pltpu.SMEM),
            pl.BlockSpec(memory_space=pltpu.SMEM),
            pl.BlockSpec(memory_space=pltpu.VMEM),
            pl.BlockSpec(memory_space=pltpu.VMEM),
        ],
        out_specs=pl.BlockSpec((angles, jr, 16, full), lambda g: (0, 0, g, 0)),
        scratch_shapes=[
            pltpu.VMEM((2, jr, nz, full), F32),
            pltpu.VMEM((tables * angles, lags * 8), jnp.bfloat16),
            pltpu.VMEM((jr * 2, 2 * LAG_REACH, 8, full), F32),
        ],
        name="image",
    )(lag_offsets, table_index, cols, lag_tables)
    return image.reshape(angles, cols_per, full)


def solution(mesh):
    wave = P(None, ("shot", "gx"), None, None)
    cell = P("gx", None, None)
    return jax.shard_map(
        local,
        mesh=mesh,
        in_specs=(wave, wave, cell, cell, cell, cell, P(), P(), P()),
        out_specs=P(None, ("shot", "gx"), None),
        check_vma=False,
    )
```

```python
import functools
import jax
import jax.numpy as jnp
from jax import lax
from jax.experimental import pallas as pl
from jax.experimental.pallas import tpu as pltpu
from jax.sharding import PartitionSpec as P

STEPS = 4
LAG_REACH = 16
PAD = 8
F32 = jnp.float32
SEND = jnp.bfloat16


def sin_cos(x):
    h = x * 0.5
    h2 = h * h
    s = h2 * 2.609020676498479e-06 + (-0.00019811149207883466)
    s = s * h2 + 0.008333088613525165
    s = s * h2 + (-0.16666660477455342)
    s = s * h2 * h + h
    c = h2 * (-2.607799327383753e-07) + 2.4761934264809493e-05
    c = c * h2 + (-0.0013888404392126607)
    c = c * h2 + 0.04166664079116777
    c = c * h2 + (-0.4999999955092854)
    c = c * h2 + 1.0
    s2 = s + s
    return s2 * c, 1.0 - s2 * s


def wave_kernel(
    n, jr, cols_per, now_hbm, prev_hbm, eps_hbm, tilt_hbm, azi_hbm, cou_hbm, cols_ref,
    buf0, buf1, dz, dy, part, eps, tilt, azi, cou, coef, pair, snap, snap_send, sendbuf, halo,
    in_sems, hs_sems, hr_sems, as_sems, ar_sems,
):
    width = eps.shape[0]
    ny = eps.shape[1]
    nz = eps.shape[2]
    rows = pl.ds(PAD, ny)
    up_rows = pl.ds(PAD + 1, ny)
    dn_rows = pl.ds(PAD - 1, ny)
    me = lax.axis_index("gx")
    has_low = me > 0
    has_high = me < n - 1
    bufs = (buf0, buf1)

    copies = [
        pltpu.make_async_copy(tilt_hbm, tilt, in_sems.at[0]),
        pltpu.make_async_copy(azi_hbm, azi, in_sems.at[1]),
        pltpu.make_async_copy(eps_hbm, eps, in_sems.at[2]),
        pltpu.make_async_copy(cou_hbm, cou, in_sems.at[3]),
        pltpu.make_async_copy(now_hbm, buf0.at[:, pl.ds(1, width), rows, :], in_sems.at[4]),
        pltpu.make_async_copy(prev_hbm, buf1.at[:, pl.ds(1, width), rows, :], in_sems.at[5]),
    ]
    for copy in copies:
        copy.start()

    barrier = pltpu.get_barrier_semaphore()

    def greet(k, carry):
        pl.semaphore_signal(
            barrier, inc=1, device_id={"gx": lax.rem(me + k, n)},
            device_id_type=pl.DeviceIdType.MESH,
        )
        return carry

    lax.fori_loop(1, n, greet, 0)

    zero_rows = jnp.zeros((2, width + 2, PAD, nz), F32)
    for ref in (buf0, buf1, dz):
        ref[:, :, pl.ds(0, PAD), :] = zero_rows
        ref[:, :, pl.ds(PAD + ny, PAD), :] = zero_rows
    zero_plane = jnp.zeros((2, ny, nz), F32)
    for plane in (0, width + 1):
        for ref in (buf0, buf1):
            ref[:, plane, rows, :] = zero_plane
        dz[:, plane, rows, :] = zero_plane
        dy[:, plane] = zero_plane

    pl.semaphore_wait(barrier, n - 1)

    def halo_copy(step, side):
        if step == 0:
            src = now_hbm.at[:, 0 if side == 0 else width - 1]
        else:
            src = sendbuf.at[step - 1, side]
        return pltpu.make_async_remote_copy(
            src_ref=src,
            dst_ref=halo.at[step, 1 - side],
            send_sem=hs_sems.at[step, side],
            recv_sem=hr_sems.at[step, 1 - side],
            device_id={"gx": me - 1 if side == 0 else me + 1},
            device_id_type=pl.DeviceIdType.MESH,
        )

    def halo_arrived(step, side):
        return pltpu.make_async_remote_copy(
            src_ref=sendbuf.at[0, side],
            dst_ref=halo.at[step, side],
            send_sem=hs_sems.at[step, side],
            recv_sem=hr_sems.at[step, side],
            device_id={"gx": me - 1 if side == 0 else me + 1},
            device_id_type=pl.DeviceIdType.MESH,
        )

    def send_halo(step):
        @pl.when(has_low)
        def _():
            halo_copy(step, 0).start()

        @pl.when(has_high)
        def _():
            halo_copy(step, 1).start()

    send_halo(0)

    for copy in copies[:4]:
        copy.wait()

    def make_coef(x, carry):
        theta_s, theta_c = sin_cos(tilt[x].astype(F32))
        alpha_s, alpha_c = sin_cos(azi[x].astype(F32))
        speed = cou[x].astype(F32)
        e2 = eps[x].astype(F32) * 2.0
        scaled = speed * e2
        base = speed + scaled
        nx = theta_s * alpha_c
        nyy = theta_s * alpha_s
        sx = scaled * nx
        sy = scaled * nyy
        scz = scaled * theta_c
        mxx = base - sx * nx
        myy = base - sy * nyy
        mzz = base - scz * theta_c
        coef[0, x] = mxx
        coef[1, x] = myy
        coef[2, x] = mzz
        coef[3, x] = -0.5 * (sx * nyy)
        coef[4, x] = -0.5 * (scz * nx)
        coef[5, x] = -0.5 * (scz * nyy)
        coef[6, x] = 2.0 - 2.0 * (mxx + myy + mzz)
        return carry

    lax.fori_loop(0, width, make_coef, 0)
    for copy in copies[4:]:
        copy.wait()

    chunk = 16
    starts = range(0, ny, chunk)

    def z_shifts(p):
        lane = lax.broadcasted_iota(jnp.int32, p.shape, 1)
        up = jnp.where(lane == nz - 1, 0.0, pltpu.roll(p, nz - 1, axis=1))
        dn = jnp.where(lane == 0, 0.0, pltpu.roll(p, 1, axis=1))
        return up, dn

    def turns(now, x, y):
        return [z_shifts(now[f, x, pl.ds(PAD + y, chunk), :]) for f in range(2)]

    def own_rows(now, x, y, turned):
        here = pl.ds(y, chunk)
        c1, c2, c6 = [coef[k, x - 1, here, :] for k in (1, 2, 6)]
        for f in range(2):
            p = now[f, x, pl.ds(PAD + y, chunk), :]
            pu = now[f, x, pl.ds(PAD + y + 1, chunk), :]
            pd = now[f, x, pl.ds(PAD + y - 1, chunk), :]
            up, dn = turned[f]
            part[f, x, here, :] = c6 * p + c1 * (pu + pd) + c2 * (up + dn)
            dz[f, x, pl.ds(PAD + y, chunk), :] = up - dn
            dy[f, x, here, :] = pu - pd

    def own_plane(now, x):
        for y in starts:
            own_rows(now, x, y, turns(now, x, y))

    def update(now, prv, x, picked=starts):
        for y in picked:
            here = pl.ds(y, chunk)
            mid = pl.ds(PAD + y, chunk)
            c0, c3, c4, c5 = [coef[k, x - 1, here, :] for k in (0, 3, 4, 5)]
            for f in range(2):
                acc = part[f, x, here, :] - prv[f, x, mid, :]
                acc += c0 * (now[f, x + 1, mid, :] + now[f, x - 1, mid, :])
                acc += c3 * (dy[f, x + 1, here, :] - dy[f, x - 1, here, :])
                acc += c4 * (dz[f, x + 1, mid, :] - dz[f, x - 1, mid, :])
                acc += c5 * (
                    dz[f, x, pl.ds(PAD + y + 1, chunk), :] - dz[f, x, pl.ds(PAD + y - 1, chunk), :]
                )
                prv[f, x, mid, :] = acc

    for step in range(STEPS):
        now, prv = bufs[step % 2], bufs[(step + 1) % 2]
        for x in (1, 2, 3):
            own_plane(now, x)

        def interior(x, carry, now=now, prv=prv):
            turned = turns(now, x + 2, 0)
            for y in starts:
                update(now, prv, x, (y,))
                ahead = turns(now, x + 2, y + chunk) if y + chunk < ny else None
                own_rows(now, x + 2, y, turned)
                turned = ahead
            return carry

        lax.fori_loop(2, width - 1, interior, 0)
        update(now, prv, width - 1)

        for side, plane, edge, has in (
            (0, 0, 1, has_low), (1, width + 1, width, has_high),
        ):
            @pl.when(has)
            def _(side=side, plane=plane, now=now, step=step):
                halo_arrived(step, side).wait_recv()
                for f in range(2):
                    p = halo[step, side, f]
                    now[f, plane, rows, :] = p
                    up, dn = z_shifts(p)
                    dz[f, plane, rows, :] = up - dn
                for f in range(2):
                    dy[f, plane] = now[f, plane, up_rows, :] - now[f, plane, dn_rows, :]

            update(now, prv, edge)
            if step < STEPS - 1:
                for f in range(2):
                    sendbuf[step, side, f] = prv[f, edge, rows, :]

                @pl.when(has)
                def _(side=side, step=step):
                    halo_copy(step + 1, side).start()

    final = bufs[STEPS % 2]
    half = width // 2

    def make_snap(i, carry):
        for f in range(2):
            pair[f] = final[f, 2 * i + 1, rows, :] + final[f, 2 * i + 2, rows, :]
        for f in range(2):
            even = pair[f, pl.ds(0, ny // 2, stride=2), :]
            odd = pair[f, pl.ds(1, ny // 2, stride=2), :]
            snap[f, pl.ds(i, ny // 2, stride=half), :] = (even + odd) * 0.25
        return carry

    lax.fori_loop(0, half, make_snap, 0)

    span = jr * half

    def piece(target, source):
        start = pl.multiple_of(((target * cols_per) // nz) * half, half)
        return pltpu.make_async_remote_copy(
            src_ref=snap_send.at[:, pl.ds(start, span), :],
            dst_ref=cols_ref.at[source],
            send_sem=as_sems.at[target],
            recv_sem=ar_sems.at[source],
            device_id={"gx": target},
            device_id_type=pl.DeviceIdType.MESH,
        )

    snap_send[...] = snap[...].astype(SEND)

    def send_piece(k, carry):
        piece(lax.rem(me + k, n), me).start()
        return carry

    lax.fori_loop(n // 2, n, send_piece, 0)
    lax.fori_loop(1, n // 2, send_piece, 0)
    start = pl.multiple_of(((me * cols_per) // nz) * half, half)
    own = pltpu.make_async_copy(snap_send.at[:, pl.ds(start, span), :], cols_ref.at[me], in_sems.at[6])
    own.start()

    for step in range(STEPS):
        @pl.when(has_low)
        def _(step=step):
            halo_copy(step, 0).wait_send()

        @pl.when(has_high)
        def _(step=step):
            halo_copy(step, 1).wait_send()

    def wait_piece(k, carry):
        piece(lax.rem(me + k, n), me).wait_send()
        piece(lax.rem(me + k, n), lax.rem(me + k, n)).wait_recv()
        return carry

    lax.fori_loop(1, n, wait_piece, 0)
    own.wait()


def image_kernel(
    cols_per, jr, offsets, tables_at, cols_ref, tab_ref, out_ref, lines, wide, prods
):
    n = cols_ref.shape[0]
    half = cols_ref.shape[2] // jr
    nz = cols_ref.shape[3]
    full = n * half
    step = pl.program_id(0)
    tables = tab_ref.shape[0]
    angles = tab_ref.shape[1]
    lags = tab_ref.shape[2]

    @pl.when(step == 0)
    def _():
        for f in range(2):
            for j in range(jr):
                for t in range(full // nz):
                    per = nz // half
                    block = cols_ref[pl.ds(t * per, per), f, pl.ds(j * half, half), :]
                    block = block.reshape(nz, nz).astype(F32)
                    lines[f, j, :, pl.ds(t * nz, nz)] = block.T.astype(SEND)
        lag = lax.broadcasted_iota(jnp.int32, (lags, lags * 8), 0)
        col = lax.broadcasted_iota(jnp.int32, (lags, lags * 8), 1)
        spread = jnp.where(col // 8 == lag, 1.0, 0.0).astype(jnp.bfloat16)
        flat = tab_ref[...].reshape(tables * angles, lags)
        wide[...] = jnp.dot(flat, spread, preferred_element_type=F32).astype(jnp.bfloat16)

    me = lax.axis_index("gx")
    z0 = lax.rem(me * cols_per, nz)
    lane = lax.broadcasted_iota(jnp.int32, (16, nz), 1)
    tiles = full // nz
    ta = tables * angles
    sub = lax.broadcasted_iota(jnp.int32, (8, ta), 0)
    row_c = lax.rem(lax.broadcasted_iota(jnp.int32, (angles * 8, lags * 8), 0), 8)
    col_c = lax.rem(lax.broadcasted_iota(jnp.int32, (angles * 8, lags * 8), 1), 8)
    diagonal = row_c == col_c
    lane_ta = lax.broadcasted_iota(jnp.int32, (angles, 8, ta), 2)
    row_a = lax.broadcasted_iota(jnp.int32, (angles, 8, ta), 0)
    weights = []
    for q in range(2):
        row0 = z0 + step * 16 + q * 8
        chosen = jnp.zeros((8, ta), jnp.int32)
        for c in range(8):
            chosen = jnp.where(sub == c, tables_at[row0 + c], chosen)
        wanted = (chosen * angles)[None] + row_a
        pick = jnp.where(lane_ta == wanted, 1.0, 0.0).reshape(angles * 8, ta)
        dense = jnp.dot(pick.astype(jnp.bfloat16), wide[...], preferred_element_type=F32)
        weights.append(jnp.where(diagonal, dense, 0.0).astype(jnp.bfloat16))

    def moved(parts, d):
        if d == 0:
            return [part.astype(F32) for part in parts]
        turned = [pltpu.roll(part, d % nz, axis=1).astype(F32) for part in parts]
        zero = jnp.zeros((16, nz), F32)
        if d > 0:
            return [
                jnp.where(lane >= d, turned[t], turned[t - 1] if t else zero)
                for t in range(tiles)
            ]
        return [
            jnp.where(lane < nz + d, turned[t], turned[t + 1] if t + 1 < tiles else zero)
            for t in range(tiles)
        ]

    for j in range(jr):
        results = []
        row0 = pl.multiple_of(z0 + step * 16, 16)
        source = [lines[0, j, pl.ds(row0, 16), pl.ds(t * nz, nz)] for t in range(tiles)]
        receiver = [lines[1, j, pl.ds(row0, 16), pl.ds(t * nz, nz)] for t in range(tiles)]
        for d in range(-LAG_REACH, LAG_REACH):
            left, right = moved(source, d), moved(receiver, -d)
            for t in range(tiles):
                product = left[t] * right[t]
                for q in range(2):
                    prods[j * 2 + q, d + LAG_REACH, :, pl.ds(t * nz, nz)] = product[8 * q : 8 * q + 8]
        for q in range(2):
            slot = j * 2 + q
            lagged = jnp.concatenate(
                [prods[slot, offsets[h] + LAG_REACH] for h in range(lags)], axis=0
            ).astype(jnp.bfloat16)
            total = jnp.dot(weights[q], lagged, preferred_element_type=F32)
            results.append(total.reshape(angles, 8, full))
        both = jnp.concatenate(results, axis=1)
        out_ref[:, j] = both.astype(jnp.bfloat16)


def local(
    waves_now, waves_prev, epsilon, tilt, azimuth, courant, lag_offsets, table_index, lag_tables
):
    n = lax.axis_size("gx")
    width, ny, nz = epsilon.shape
    half = width // 2
    columns = (ny // 2) * nz
    cols_per = columns // n
    jr = max(1, cols_per // nz)
    full = n * half
    plane = (2, width + 2, ny + 2 * PAD, nz)
    dma = pltpu.SemaphoreType.DMA
    cols = pl.pallas_call(
        functools.partial(wave_kernel, n, jr, cols_per),
        out_shape=jax.ShapeDtypeStruct((n, 2, jr * half, nz), SEND),
        in_specs=[pl.BlockSpec(memory_space=pl.ANY)] * 6,
        out_specs=pl.BlockSpec(memory_space=pltpu.VMEM),
        scratch_shapes=[
            pltpu.VMEM(plane, F32),
            pltpu.VMEM(plane, F32),
            pltpu.VMEM(plane, F32),
            pltpu.VMEM((2, width + 2, ny, nz), F32),
            pltpu.VMEM((2, width + 2, ny, nz), F32),
            pltpu.VMEM((width, ny, nz), epsilon.dtype),
            pltpu.VMEM((width, ny, nz), tilt.dtype),
            pltpu.VMEM((width, ny, nz), azimuth.dtype),
            pltpu.VMEM((width, ny, nz), courant.dtype),
            pltpu.VMEM((7, width, ny, nz), F32),
            pltpu.VMEM((2, ny, nz), F32),
            pltpu.VMEM((2, (ny // 2) * half, nz), F32),
            pltpu.VMEM((2, (ny // 2) * half, nz), SEND),
            pltpu.VMEM((STEPS - 1, 2, 2, ny, nz), F32),
            pltpu.VMEM((STEPS, 2, 2, ny, nz), F32),
            dma((7,)),
            dma((STEPS, 2)),
            dma((STEPS, 2)),
            dma((n,)),
            dma((n,)),
        ],
        compiler_params=pltpu.CompilerParams(collective_id=0, has_side_effects=True),
        name="waves",
    )(waves_now, waves_prev, epsilon, tilt, azimuth, courant)

    angles, lags = lag_tables.shape[1:]
    tables = lag_tables.shape[0]
    cz = min(cols_per, nz)
    image = pl.pallas_call(
        functools.partial(image_kernel, cols_per, jr),
        grid=(cz // 16,),
        out_shape=jax.ShapeDtypeStruct((angles, jr, cz, full), jnp.bfloat16),
        in_specs=[
            pl.BlockSpec(memory_space=pltpu.SMEM),
            pl.BlockSpec(memory_space=pltpu.SMEM),
            pl.BlockSpec(memory_space=pltpu.VMEM),
            pl.BlockSpec(memory_space=pltpu.VMEM),
        ],
        out_specs=pl.BlockSpec((angles, jr, 16, full), lambda g: (0, 0, g, 0)),
        scratch_shapes=[
            pltpu.VMEM((2, jr, nz, full), SEND),
            pltpu.VMEM((tables * angles, lags * 8), jnp.bfloat16),
            pltpu.VMEM((jr * 2, 2 * LAG_REACH, 8, full), F32),
        ],
        name="image",
    )(lag_offsets, table_index, cols, lag_tables)
    return image.reshape(angles, cols_per, full)


def solution(mesh):
    wave = P(None, ("shot", "gx"), None, None)
    cell = P("gx", None, None)
    return jax.shard_map(
        local,
        mesh=mesh,
        in_specs=(wave, wave, cell, cell, cell, cell, P(), P(), P()),
        out_specs=P(None, ("shot", "gx"), None),
        check_vma=False,
    )
```
